256 devices in a mesh: replica: 64 (over y, z, core), tensor: 4 (over x).
Axes of the slice: x: 4, y: 4, z: 8, core: 2. Of those that a mesh axis runs over, the one named last changes fastest.
Arguments:
- grad_q: bfloat16 [131072, 2048], P('replica', 'tensor'), may hold values from -6 to 6
- error_q: bfloat16 [131072, 2048], P('replica', 'tensor'), may hold values from -6 to 6
- qfac_q: bfloat16 [2048, 32], P('tensor'), may hold values from -0.25 to 0.25
- ginv_q: float32 [128, 32], P('tensor'), as said below
- weight_q: float32 [2048, 2048], P('replica', 'tensor'), may hold values from -6 to 6
- momentum_q: float32 [2048, 2048], P('replica', 'tensor'), may hold values from -4 to 4
- grad_o: bfloat16 [131072, 2048], P(('replica', 'tensor')), may hold values from -6 to 6
- error_o: bfloat16 [131072, 2048], P(('replica', 'tensor')), may hold values from -6 to 6
- qfac_o: bfloat16 [8192, 32], P('tensor'), may hold values from -0.125 to 0.125
- ginv_o: float32 [128, 32], P('tensor'), as said below
- weight_o: float32 [2048, 2048], P('tensor', 'replica'), may hold values from -6 to 6
- momentum_o: float32 [2048, 2048], P('tensor', 'replica'), may hold values from -4 to 4
- norm_grads: bfloat16 [64, 4, 4096], P('replica', 'tensor'), may hold values from -24 to 24
Outputs:
- error_q_new: bfloat16 [131072, 2048], P('replica', 'tensor')
- qfac_q_new: bfloat16 [2048, 32], P('tensor')
- momentum_q_new: float32 [2048, 2048], P('replica', 'tensor')
- weight_q_new: float32 [2048, 2048], P('replica', 'tensor')
- error_o_new: bfloat16 [131072, 2048], P(('replica', 'tensor'))
- qfac_o_new: bfloat16 [8192, 32], P('tensor')
- momentum_o_new: float32 [2048, 2048], P('tensor', 'replica')
- weight_o_new: float32 [2048, 2048], P('tensor', 'replica')
- norm_mean: float32 [4096], replicated
The draws below stay inside these ranges and needn't reach their ends.
Inputs may be any that keep to these rules, and one draw needn't show every extreme that they name: `ginv_q`: each block of 32 rows is an upper-triangular matrix with a positive diagonal. `ginv_o`: each block of 32 rows is an upper-triangular matrix with a positive diagonal.
All inputs are finite; a program needn't handle non-finite values.
Results may differ from the reference program's by a relative error of at most 0.0085.
Values may be sent and summed in bfloat16 or wider, within the bound.
A program may use at most 64 MiB of HBM per device.

```python
import jax
import jax.numpy as jnp
from jax import lax

D = 2048
HD = 2048
RANK = 32
REPLICAS = 64
N_REPLICA = 64
N_TENSOR = 4


def gram_factor(key, row_count):
    key_diag, key_off = jax.random.split(key)
    diagonal = jnp.exp(jax.random.uniform(key_diag, (N_TENSOR, RANK), jnp.float32, jnp.log(0.7), jnp.log(1.4)))
    offdiag = 0.35 * jax.random.truncated_normal(key_off, -3.0, 3.0, (N_TENSOR, RANK, RANK), jnp.float32) / jnp.sqrt(jnp.float32(RANK))
    row_ids = jnp.arange(RANK)[:, None]
    col_ids = jnp.arange(RANK)[None, :]
    upper = (col_ids > row_ids).astype(jnp.float32)
    ident = (col_ids == row_ids).astype(jnp.float32)
    matrix = offdiag * upper[None] + diagonal[:, :, None] * ident[None]
    scale_value = 1.5 / jnp.sqrt(jnp.float32(row_count * REPLICAS))
    return (matrix * scale_value).reshape(N_TENSOR * RANK, RANK)


def draw_ginv_q(key, part):
    return gram_factor(jax.random.fold_in(key, 11), D)


def draw_ginv_o(key, part):
    return gram_factor(jax.random.fold_in(key, 23), HD // N_TENSOR)


def block_scale(stream_key, shape, cuts, smallest, largest):
    loudness = 1.0
    for dim, blocks in cuts:
        steps = jax.random.uniform(jax.random.fold_in(jax.random.fold_in(stream_key, 6), dim), (blocks,), jnp.float32, smallest / len(cuts), largest / len(cuts))
        loudness = loudness * jnp.repeat(jnp.exp(steps), shape[dim] // blocks).reshape((-1,) + (1,) * (len(shape) - 1 - dim))
    return loudness


def gaussian(stream_key, shape, spread, most, cuts=(), dtype=jnp.bfloat16):
    level = block_scale(stream_key, shape, cuts, -0.22, 0.18) if cuts else 1.0
    result = jax.random.normal(stream_key, shape, jnp.float32) * spread * level
    return jnp.minimum(jnp.maximum(result, -most), most).astype(dtype)


def setup_inputs(seed: int = 0) -> dict:
    key_list = jax.random.split(jax.random.key(seed), 14)
    return {
        "grad_q": gaussian(key_list[0], (N_REPLICA * D, HD), 1.0, 6.0, ((0, 64), (1, 4))),
        "error_q": gaussian(key_list[1], (N_REPLICA * D, HD), 0.5, 6.0, ((0, 64), (1, 4))),
        "qfac_q": gaussian(key_list[2], (HD, RANK), (HD // N_TENSOR) ** -0.5, 0.25, ((0, 4),)),
        "ginv_q": draw_ginv_q(jax.random.fold_in(key_list[13], 71), 0),
        "weight_q": gaussian(key_list[4], (D, HD), 1.0, 6.0, ((0, 64), (1, 4)), jnp.float32),
        "momentum_q": gaussian(key_list[5], (D, HD), 0.3, 4.0, ((0, 64), (1, 4)), jnp.float32),
        "grad_o": gaussian(key_list[6], (N_REPLICA * HD, D), 1.0, 6.0, ((0, 256),)),
        "error_o": gaussian(key_list[7], (N_REPLICA * HD, D), 0.5, 6.0, ((0, 256),)),
        "qfac_o": gaussian(key_list[8], (N_TENSOR * D, RANK), D ** -0.5, 0.125, ((0, 4),)),
        "ginv_o": draw_ginv_o(jax.random.fold_in(key_list[13], 71), 0),
        "weight_o": gaussian(key_list[10], (HD, D), 1.0, 6.0, ((0, 4), (1, 64)), jnp.float32),
        "momentum_o": gaussian(key_list[11], (HD, D), 0.3, 4.0, ((0, 4), (1, 64)), jnp.float32),
        "norm_grads": gaussian(key_list[12], (N_REPLICA, N_TENSOR, 2 * D), 4.0, 24.0, ((0, 64), (1, 4))),
    }


momentum_decay = 0.9
step_size = 0.5


def sum_replicas(term, mat_all):
    first = term(mat_all[0])

    def accumulate(running, matrix):
        return running + term(matrix), None

    return lax.scan(accumulate, jnp.zeros_like(first), mat_all)[0]


def compress_shard(grads, errors, qfac, ginv):
    mat_all = (grads.astype(jnp.float32) + errors.astype(jnp.float32)).astype(jnp.bfloat16)
    p_sum = sum_replicas(lambda matrix: jnp.dot(matrix, qfac, preferred_element_type=jnp.float32), mat_all)
    p_hat = jnp.dot(p_sum, ginv, precision=lax.Precision.HIGHEST).astype(jnp.bfloat16)
    q_sum = sum_replicas(lambda matrix: lax.dot_general(matrix, p_hat, (((0,), (0,)), ((), ())), preferred_element_type=jnp.float32), mat_all)
    q_new = (q_sum / N_REPLICA).astype(jnp.bfloat16)
    approx = lax.dot_general(p_hat, q_new, (((1,), (1,)), ((), ())), preferred_element_type=jnp.float32)
    err_new = (mat_all.astype(jnp.float32) - approx[None]).astype(jnp.bfloat16)
    return err_new, q_new, approx


def reference(grad_q, error_q, qfac_q, ginv_q, weight_q, momentum_q, grad_o, error_o, qfac_o, ginv_o, weight_o, momentum_o, norm_grads):
    local_width = HD // N_TENSOR
    grad_q3 = grad_q.reshape(N_REPLICA, D, HD)
    error_q3 = error_q.reshape(N_REPLICA, D, HD)
    grad_o3 = grad_o.reshape(N_REPLICA, HD, D)
    error_o3 = error_o.reshape(N_REPLICA, HD, D)
    errs_q, facs_q, apps_q = [], [], []
    errs_o, facs_o, apps_o = [], [], []
    for shard_index in range(N_TENSOR):
        low = shard_index * local_width
        gram_q = ginv_q[shard_index * RANK:(shard_index + 1) * RANK]
        gram_o = ginv_o[shard_index * RANK:(shard_index + 1) * RANK]
        err_new, q_new, approx = compress_shard(grad_q3[:, :, low:low + local_width], error_q3[:, :, low:low + local_width], qfac_q[low:low + local_width], gram_q)
        errs_q.append(err_new)
        facs_q.append(q_new)
        apps_q.append(approx)
        err_new, q_new, approx = compress_shard(grad_o3[:, low:low + local_width], error_o3[:, low:low + local_width], qfac_o[shard_index * D:(shard_index + 1) * D], gram_o)
        errs_o.append(err_new)
        facs_o.append(q_new)
        apps_o.append(approx)
    error_q_new = jnp.concatenate(errs_q, axis=2).reshape(N_REPLICA * D, HD)
    qfac_q_new = jnp.concatenate(facs_q, axis=0)
    approx_q = jnp.concatenate(apps_q, axis=1)
    error_o_new = jnp.concatenate(errs_o, axis=1).reshape(N_REPLICA * HD, D)
    qfac_o_new = jnp.concatenate(facs_o, axis=0)
    approx_o = jnp.concatenate(apps_o, axis=0)
    momentum_q_new = momentum_decay * momentum_q + approx_q
    weight_q_new = weight_q - step_size * momentum_q_new
    momentum_o_new = momentum_decay * momentum_o + approx_o
    weight_o_new = weight_o - step_size * momentum_o_new
    norm_mean = jnp.sum(norm_grads.astype(jnp.float32), axis=(0, 1)) / (N_REPLICA * N_TENSOR)
    return (error_q_new, qfac_q_new, momentum_q_new, weight_q_new, error_o_new, qfac_o_new, momentum_o_new, weight_o_new, norm_mean)
```

```python
import functools

import jax
import jax.numpy as jnp
from jax import lax
from jax.experimental import pallas as pl
from jax.experimental.pallas import tpu as pltpu
from jax.sharding import PartitionSpec as P

momentum_decay = 0.9
step_size = 0.5

NY, NZ, NC = 4, 8, 2
NA = NY * NC
RANK = 32
TILES = 5
MESH = pl.DeviceIdType.MESH
f32 = jnp.float32
bf16 = jnp.bfloat16

A_FAR = [(2, 0), (2, 1), (1, 0), (3, 0), (1, 1), (3, 1), (0, 1)]
A_NEAR = A_FAR[::-1]
Z_FAR = [4, 3, 5, 2, 6, 1, 7]


def fold_gram(gram, factor_t):
    w = lax.dot_general(
        gram,
        factor_t.astype(f32),
        (((0,), (0,)), ((), ())),
        precision=lax.Precision.HIGHEST,
        preferred_element_type=f32,
    )
    w1 = w.astype(bf16)
    r1 = w - w1.astype(f32)
    w2 = r1.astype(bf16)
    w3 = (r1 - w2.astype(f32)).astype(bf16)
    return w1, w2, w3


def project(w, mat):
    out = lax.dot_general(w, mat, (((1,), (1,)), ((), ())), preferred_element_type=f32)
    return out[0:RANK] + out[RANK : 2 * RANK] + out[2 * RANK : 3 * RANK]


def wide_tiles(chunk):
    return [chunk[h * 16 : h * 16 + 16, j * 128 : j * 128 + 128] for h in range(2) for j in range(2)]


def reduce_kernel(
    replicas,
    all_devices,
    gq,
    eq,
    go,
    eo,
    fq,
    fo,
    giq,
    gio,
    nrm,
    matq_out,
    mato_out,
    gp_out,
    gn_out,
    norm_out,
    gq_v,
    eq_v,
    go_v,
    eo_v,
    mq,
    mo,
    fq_v,
    fo_v,
    giq_v,
    gio_v,
    nrm_v,
    wq,
    wo,
    send_a,
    recv_a,
    zbuf,
    gath,
    nsrc,
    nrecv,
    nz,
    nx,
    ng,
    sem_q,
    sem_o,
    sem_s,
    sem_w,
    sem_as,
    sem_ar,
    sem_zs,
    sem_zr,
    sem_gs,
    sem_gr,
    nsem_as,
    nsem_ar,
    nsem_zs,
    nsem_zr,
    nsem_xs,
    nsem_xr,
    nsem_gs,
    nsem_gr,
):
    rep = lax.axis_index("replica")
    ten = lax.axis_index("tensor")
    nx_size = lax.axis_size("tensor")
    y = rep // (NZ * NC)
    z = (rep // NC) % NZ
    core = rep % NC
    a = y * NC + core

    def a_peer(off):
        py, pc = (y + off[0]) % NY, (core + off[1]) % NC
        return py * NC + pc, ((py * NZ + z) * NC + pc, ten)

    def z_peer(dz):
        pz = (z + dz) % NZ
        return pz, ((y * NZ + pz) * NC + core, ten)

    def x_peer(dx):
        px = (ten + dx) % nx_size
        return px, (rep, px)

    barrier = pltpu.get_barrier_semaphore()
    for off in A_FAR:
        pl.semaphore_signal(barrier, inc=1, device_id=a_peer(off)[1], device_id_type=MESH)
    for dz in Z_FAR:
        pl.semaphore_signal(barrier, inc=1, device_id=z_peer(dz)[1], device_id_type=MESH)
    for dx in range(1, nx_size):
        pl.semaphore_signal(barrier, inc=1, device_id=x_peer(dx)[1], device_id_type=MESH)

    small = [(fq, fq_v), (fo, fo_v), (giq, giq_v), (gio, gio_v), (nrm, nrm_v)]
    small_copies = [pltpu.make_async_copy(s, d, sem_s.at[i]) for i, (s, d) in enumerate(small)]
    for c in small_copies:
        c.start()
    o_rows = go.shape[0] // 4
    q_rows = gq.shape[0] // NA

    def o_loads(j):
        rows = pl.ds(j * o_rows, o_rows)
        return [
            pltpu.make_async_copy(go.at[rows, :], go_v.at[rows, :], sem_o.at[0, j]),
            pltpu.make_async_copy(eo.at[rows, :], eo_v.at[rows, :], sem_o.at[1, j]),
        ]

    def q_slice(d):
        return pl.ds(pl.multiple_of(d * q_rows, q_rows), q_rows)

    def q_loads(d):
        rows = q_slice(d)
        return [
            pltpu.make_async_copy(gq.at[rows, :], gq_v.at[rows, :], sem_q.at[0, d]),
            pltpu.make_async_copy(eq.at[rows, :], eq_v.at[rows, :], sem_q.at[1, d]),
        ]

    order = A_FAR + [(0, 0)]
    for j in range(4):
        for c in o_loads(j):
            c.start()
    for off in order:
        for c in q_loads(a_peer(off)[0]):
            c.start()

    def exchange(src, dst, send_sem, recv_sem, device):
        return pltpu.make_async_remote_copy(
            src_ref=src, dst_ref=dst, send_sem=send_sem, recv_sem=recv_sem,
            device_id=device, device_id_type=MESH,
        )

    def a_copy(ph, off):
        d, dev = a_peer(off)
        return exchange(send_a.at[ph, d], recv_a.at[ph, a], sem_as.at[ph, d], sem_ar.at[ph, a], dev)

    def a_wait(ph, off):
        d, dev = a_peer(off)
        exchange(send_a.at[ph, d], recv_a.at[ph, d], sem_as.at[ph, d], sem_ar.at[ph, d], dev).wait_recv()
        return recv_a[ph, d].astype(f32)

    def z_copy(ph, dz):
        d, dev = z_peer(dz)
        return exchange(zbuf.at[ph, z], zbuf.at[ph, z], sem_zs.at[ph, d], sem_zr.at[ph, z], dev)

    def z_wait(ph, dz):
        d, dev = z_peer(dz)
        exchange(zbuf.at[ph, d], zbuf.at[ph, d], sem_zs.at[ph, d], sem_zr.at[ph, d], dev).wait_recv()

    def g_copy(ph, off):
        d, dev = a_peer(off)
        return exchange(gath.at[ph, a], gath.at[ph, a], sem_gs.at[ph, d], sem_gr.at[ph, a], dev)

    def g_wait(ph, off):
        d, dev = a_peer(off)
        exchange(gath.at[ph, d], gath.at[ph, d], sem_gs.at[ph, d], sem_gr.at[ph, d], dev).wait_recv()
        return d

    def na_copy(off):
        d, dev = a_peer(off)
        return exchange(nsrc.at[d], nrecv.at[a], nsem_as.at[d], nsem_ar.at[a], dev)

    def na_wait(off):
        d, dev = a_peer(off)
        exchange(nsrc.at[d], nrecv.at[d], nsem_as.at[d], nsem_ar.at[d], dev).wait_recv()
        return nrecv[d]

    def nz_copy(dz):
        d, dev = z_peer(dz)
        return exchange(nz.at[z], nz.at[z], nsem_zs.at[d], nsem_zr.at[z], dev)

    def nz_wait(dz):
        d, dev = z_peer(dz)
        exchange(nz.at[d], nz.at[d], nsem_zs.at[d], nsem_zr.at[d], dev).wait_recv()

    def nx_copy(dx):
        d, dev = x_peer(dx)
        return exchange(nx.at[ten], nx.at[ten], nsem_xs.at[d], nsem_xr.at[ten], dev)

    def nx_wait(dx):
        d, dev = x_peer(dx)
        exchange(nx.at[d], nx.at[d], nsem_xs.at[d], nsem_xr.at[d], dev).wait_recv()

    def ng_copy(off):
        d, dev = a_peer(off)
        return exchange(ng.at[a], ng.at[a], nsem_gs.at[d], nsem_gr.at[a], dev)

    def ng_wait(off):
        d, dev = a_peer(off)
        exchange(ng.at[d], ng.at[d], nsem_gs.at[d], nsem_gr.at[d], dev).wait_recv()

    for c in small_copies:
        c.wait()
    for i, w in enumerate(fold_gram(gio_v[...], fo_v[...])):
        wo[i * RANK : (i + 1) * RANK, :] = w
    for i, w in enumerate(fold_gram(giq_v[...], fq_v[...])):
        wq[i * RANK : (i + 1) * RANK, :] = w
    piece = nsrc.shape[2]
    for d in range(NA):
        nsrc[d] = nrm_v[0, :, d * piece : (d + 1) * piece].astype(f32)

    stores = []
    for j in range(4):
        for c in o_loads(j):
            c.wait()
        rows = pl.ds(j * o_rows, o_rows)
        mat = (go_v[rows, :].astype(f32) + eo_v[rows, :].astype(f32)).astype(bf16)
        mo[rows, :] = mat
        part = project(wo[...], mat).astype(bf16)
        send_a[0, j, 4] = part[0:16]
        send_a[0, 4 + j, 4] = part[16:32]
        c = pltpu.make_async_copy(mo.at[rows, :], mato_out.at[rows, :], sem_w.at[1, j])
        c.start()
        stores.append(c)

    n_others = len(A_FAR) + len(Z_FAR) + nx_size - 1
    pl.semaphore_wait(barrier, n_others)
    for off in A_FAR:
        na_copy(off).start()

    for off in order:
        d, _ = a_peer(off)
        for c in q_loads(d):
            c.wait()
        rows = q_slice(d)
        mat = (gq_v[rows, :].astype(f32) + eq_v[rows, :].astype(f32)).astype(bf16)
        mq[rows, :] = mat
        part = project(wq[...], mat).astype(bf16)
        for t, tile in enumerate(wide_tiles(part)):
            send_a[0, d, t] = tile
        if off != (0, 0):
            a_copy(0, off).start()
        c = pltpu.make_async_copy(mq.at[rows, :], matq_out.at[rows, :], sem_w.at[0, d])
        c.start()
        stores.append(c)

    def sum_a(ph):
        total = send_a[ph, a].astype(f32)
        for off in A_NEAR:
            total = total + a_wait(ph, off)
        zbuf[ph, z] = total.astype(bf16)
        for dz in Z_FAR:
            z_copy(ph, dz).start()

    def sum_z(ph, divisor):
        for dz in Z_FAR[::-1]:
            z_wait(ph, dz)
        total = zbuf[ph, 0].astype(f32)
        for k in range(1, NZ):
            total = total + zbuf[ph, k].astype(f32)
        if divisor is not None:
            total = total / divisor
        gath[ph, a] = total.astype(bf16)
        for off in A_FAR:
            g_copy(ph, off).start()

    ntotal = nsrc[a]
    for off in A_NEAR:
        ntotal = ntotal + na_wait(off)
    nz[z] = ntotal
    for dz in Z_FAR:
        nz_copy(dz).start()

    sum_a(0)

    for dz in Z_FAR:
        nz_wait(dz)
    ntotal = nz[0]
    for k in range(1, NZ):
        ntotal = ntotal + nz[k]
    nx[ten] = ntotal
    for dx in range(1, nx_size):
        nx_copy(dx).start()

    sum_z(0, None)

    for dx in range(1, nx_size):
        nx_wait(dx)
    ntotal = nx[0]
    for k in range(1, nx_size):
        ntotal = ntotal + nx[k]
    ng[a] = ntotal / all_devices
    for off in A_FAR:
        ng_copy(off).start()

    acc_q = jnp.zeros((RANK, mq.shape[1]), f32)
    for off in [(0, 0)] + A_NEAR:
        d = a if off == (0, 0) else g_wait(0, off)
        left = jnp.concatenate(
            [
                jnp.concatenate([gath[0, d, 0], gath[0, d, 1]], axis=1),
                jnp.concatenate([gath[0, d, 2], gath[0, d, 3]], axis=1),
            ],
            axis=0,
        )
        acc_q = acc_q + jnp.dot(left, mq[q_slice(d), :], preferred_element_type=f32)
    for d in range(NA):
        h, j = d // 4, d % 4
        send_a[1, d, 4] = acc_q[h * 16 : h * 16 + 16, j * 128 : j * 128 + 128].astype(bf16)
    left = jnp.concatenate(
        [jnp.concatenate([gath[0, 4 * h + j, 4] for j in range(4)], axis=1) for h in range(2)], axis=0
    )
    o_cols = mo.shape[1] // NA
    for off in order:
        d, _ = a_peer(off)
        cols = pl.ds(pl.multiple_of(d * o_cols, o_cols), o_cols)
        part = jnp.dot(left, mo[:, cols], preferred_element_type=f32).astype(bf16)
        for t, tile in enumerate(wide_tiles(part)):
            send_a[1, d, t] = tile
        if off != (0, 0):
            a_copy(1, off).start()
    gp_out[...] = gath[0]

    sum_a(1)
    for off in A_FAR:
        ng_wait(off)
    for d in range(NA):
        norm_out[:, d * piece : (d + 1) * piece] = ng[d]
    sum_z(1, replicas)
    for c in stores:
        c.wait()
    for ph in range(2):
        for off in A_FAR:
            a_copy(ph, off).wait_send()
        for dz in Z_FAR:
            z_copy(ph, dz).wait_send()
    for off in A_FAR:
        g_copy(0, off).wait_send()
        na_copy(off).wait_send()
        ng_copy(off).wait_send()
    for dz in Z_FAR:
        nz_copy(dz).wait_send()
    for dx in range(1, nx_size):
        nx_copy(dx).wait_send()
    for off in A_NEAR:
        g_wait(1, off)
    gn_out[...] = gath[1]
    for off in A_FAR:
        g_copy(1, off).wait_send()


def wide(ref, d):
    return jnp.concatenate(
        [
            jnp.concatenate([ref[d, 0], ref[d, 1]], axis=1),
            jnp.concatenate([ref[d, 2], ref[d, 3]], axis=1),
        ],
        axis=0,
    )


def narrow(ref):
    return jnp.concatenate(
        [jnp.concatenate([ref[4 * h + j, 4] for j in range(4)], axis=1) for h in range(2)], axis=0
    )


def outer(left_t, right_t):
    return lax.dot_general(left_t, right_t, (((0,), (0,)), ((), ())), preferred_element_type=f32)


def update_kernel(
    gp, gn, nrm, mq, mo, wq, mom_q, wo, mom_o,
    eq_out, eo_out, fq_out, fo_out, momq_out, wq_out, momo_out, wo_out, norm_out,
    turn,
):
    s = pl.program_id(0)
    rep = lax.axis_index("replica")
    right_q = narrow(gn)

    @pl.when(s == 0)
    def _():
        fq_out[...] = right_q
        for d in range(NA):
            fo_out[:, d * 256 : (d + 1) * 256] = wide(gn, d)
        norm_out[...] = nrm[...]
        c = rep // 8
        off = pl.multiple_of((rep % 8) * RANK, RANK)
        turn[...] = wide(gp, c).astype(f32).T
        left = turn[pl.ds(off, RANK), :].astype(bf16)
        piece = jnp.dot(left, right_q, preferred_element_type=f32)
        m = momentum_decay * mom_q[...] + piece
        momq_out[...] = m
        wq_out[...] = wq[...] - step_size * m
        turn[...] = wide(gn, c).astype(f32).T
        left = turn[pl.ds(off, RANK), :].astype(bf16)
        piece = jnp.dot(left, narrow(gp), preferred_element_type=f32)
        m = momentum_decay * mom_o[...] + piece
        momo_out[...] = m
        wo_out[...] = wo[...] - step_size * m

    for k in range(2):
        rows = slice(k * 256, (k + 1) * 256)
        approx = outer(wide(gp, 2 * s + k), right_q)
        eq_out[rows, :] = (mq[rows, :].astype(f32) - approx).astype(bf16)
    left_o = jnp.concatenate([gp[s, 4], gp[4 + s, 4]], axis=0)
    for d in range(NA):
        cols = slice(d * 256, (d + 1) * 256)
        approx = outer(left_o, wide(gn, d))
        eo_out[:, cols] = (mo[:, cols].astype(f32) - approx).astype(bf16)


def on_device(
    grad_q,
    error_q,
    qfac_q,
    ginv_q,
    weight_q,
    momentum_q,
    grad_o,
    error_o,
    qfac_o,
    ginv_o,
    weight_o,
    momentum_o,
    norm_grads,
):
    replicas = lax.axis_size("replica")
    tensors = lax.axis_size("tensor")
    shape_q, shape_o = grad_q.shape, grad_o.shape
    piece = norm_grads.shape[2] // NA
    packed = (NA, TILES, 16, 128)
    any_spec = pl.BlockSpec(memory_space=pl.ANY)
    vmem_spec = pl.BlockSpec(memory_space=pltpu.VMEM)
    dma = pltpu.SemaphoreType.DMA
    mat_q, mat_o, gp, gn, norm = pl.pallas_call(
        functools.partial(reduce_kernel, replicas, replicas * tensors),
        out_shape=(
            jax.ShapeDtypeStruct(shape_q, bf16),
            jax.ShapeDtypeStruct(shape_o, bf16),
            jax.ShapeDtypeStruct(packed, bf16),
            jax.ShapeDtypeStruct(packed, bf16),
            jax.ShapeDtypeStruct((1, NA * piece), f32),
        ),
        in_specs=[any_spec] * 9,
        out_specs=(any_spec, any_spec, vmem_spec, vmem_spec, vmem_spec),
        scratch_shapes=[
            pltpu.VMEM(shape_q, bf16),
            pltpu.VMEM(shape_q, bf16),
            pltpu.VMEM(shape_o, bf16),
            pltpu.VMEM(shape_o, bf16),
            pltpu.VMEM(shape_q, bf16),
            pltpu.VMEM(shape_o, bf16),
            pltpu.VMEM((RANK, shape_q[1]), bf16),
            pltpu.VMEM((RANK, shape_o[1]), bf16),
            pltpu.VMEM((RANK, RANK), f32),
            pltpu.VMEM((RANK, RANK), f32),
            pltpu.VMEM(norm_grads.shape, bf16),
            pltpu.VMEM((3 * RANK, shape_q[1]), bf16),
            pltpu.VMEM((3 * RANK, shape_o[1]), bf16),
            pltpu.VMEM((2,) + packed, bf16),
            pltpu.VMEM((2,) + packed, bf16),
            pltpu.VMEM((2,) + packed, bf16),
            pltpu.VMEM((2,) + packed, bf16),
            pltpu.VMEM((NA, 1, piece), f32),
            pltpu.VMEM((NA, 1, piece), f32),
            pltpu.VMEM((NZ, 1, piece), f32),
            pltpu.VMEM((tensors, 1, piece), f32),
            pltpu.VMEM((NA, 1, piece), f32),
            dma((2, NA)),
            dma((2, 4)),
            dma((5,)),
            dma((2, NA)),
            dma((2, NA)),
            dma((2, NA)),
            dma((2, NZ)),
            dma((2, NZ)),
            dma((2, NA)),
            dma((2, NA)),
            dma((NA,)),
            dma((NA,)),
            dma((NZ,)),
            dma((NZ,)),
            dma((tensors,)),
            dma((tensors,)),
            dma((NA,)),
            dma((NA,)),
        ],
        compiler_params=pltpu.CompilerParams(collective_id=0, has_side_effects=True),
        name="reduce_factors",
    )(grad_q, error_q, grad_o, error_o, qfac_q.T, qfac_o.T, ginv_q, ginv_o, norm_grads)

    steps = 4
    whole = lambda shape: pl.BlockSpec(shape, lambda s: (0,) * len(shape))
    rows_q, rows_o = shape_q[0] // steps, shape_o[0] // steps
    block_q = pl.BlockSpec((rows_q, shape_q[1]), lambda s: (s, 0))
    block_o = pl.BlockSpec((rows_o, shape_o[1]), lambda s: (s, 0))
    wide_piece = (RANK, shape_q[1])
    outs = pl.pallas_call(
        update_kernel,
        grid=(steps,),
        out_shape=(
            jax.ShapeDtypeStruct(shape_q, bf16),
            jax.ShapeDtypeStruct(shape_o, bf16),
            jax.ShapeDtypeStruct((RANK, shape_q[1]), bf16),
            jax.ShapeDtypeStruct((RANK, shape_o[1]), bf16),
            jax.ShapeDtypeStruct(wide_piece, f32),
            jax.ShapeDtypeStruct(wide_piece, f32),
            jax.ShapeDtypeStruct(wide_piece, f32),
            jax.ShapeDtypeStruct(wide_piece, f32),
            jax.ShapeDtypeStruct((1, NA * piece), f32),
        ),
        in_specs=[
            whole(packed),
            whole(packed),
            whole((1, NA * piece)),
            block_q,
            block_o,
            whole(wide_piece),
            whole(wide_piece),
            whole(wide_piece),
            whole(wide_piece),
        ],
        out_specs=(
            block_q,
            block_o,
            whole((RANK, shape_q[1])),
            whole((RANK, shape_o[1])),
            whole(wide_piece),
            whole(wide_piece),
            whole(wide_piece),
            whole(wide_piece),
            whole((1, NA * piece)),
        ),
        scratch_shapes=[pltpu.VMEM((256, RANK), f32)],
        name="apply_update",
    )(gp, gn, norm, mat_q, mat_o, weight_q, momentum_q, weight_o.T, momentum_o.T)
    error_q_new, error_o_new, fq_t, fo_t, momq, wq, momo_t, wo_t, norm_mean = outs
    return (
        error_q_new,
        fq_t.T,
        momq,
        wq,
        error_o_new,
        fo_t.T,
        momo_t.T,
        wo_t.T,
        norm_mean.reshape(-1),
    )


def solution(mesh):
    in_specs = (
        P("replica", "tensor"),
        P("replica", "tensor"),
        P("tensor", None),
        P("tensor", None),
        P("replica", "tensor"),
        P("replica", "tensor"),
        P(("replica", "tensor"), None),
        P(("replica", "tensor"), None),
        P("tensor", None),
        P("tensor", None),
        P("tensor", "replica"),
        P("tensor", "replica"),
        P("replica", "tensor", None),
    )
    out_specs = (
        P("replica", "tensor"),
        P("tensor", None),
        P("replica", "tensor"),
        P("replica", "tensor"),
        P(("replica", "tensor"), None),
        P("tensor", None),
        P("tensor", "replica"),
        P("tensor", "replica"),
        P(),
    )
    return jax.shard_map(
        on_device, mesh=mesh, in_specs=in_specs, out_specs=out_specs, check_vma=False
    )
```

```python
import functools

import jax
import jax.numpy as jnp
from jax import lax
from jax.experimental import pallas as pl
from jax.experimental.pallas import tpu as pltpu
from jax.sharding import PartitionSpec as P

momentum_decay = 0.9
step_size = 0.5

NY, NZ, NC = 4, 8, 2
NA = NY * NC
RANK = 32
TILES = 5
MESH = pl.DeviceIdType.MESH
f32 = jnp.float32
bf16 = jnp.bfloat16

A_FAR = [(2, 0), (2, 1), (1, 0), (3, 0), (1, 1), (3, 1), (0, 1)]
A_NEAR = A_FAR[::-1]
Z_FAR = [4, 3, 5, 2, 6, 1, 7]


def fold_gram(gram, factor_t):
    w = lax.dot_general(
        gram,
        factor_t.astype(f32),
        (((0,), (0,)), ((), ())),
        precision=lax.Precision.HIGHEST,
        preferred_element_type=f32,
    )
    w1 = w.astype(bf16)
    return w1, (w - w1.astype(f32)).astype(bf16)


def project(w, mat):
    out = lax.dot_general(w, mat, (((1,), (1,)), ((), ())), preferred_element_type=f32)
    return out[0:RANK] + out[RANK : 2 * RANK]


def wide_tiles(chunk):
    return [chunk[h * 16 : h * 16 + 16, j * 128 : j * 128 + 128] for h in range(2) for j in range(2)]


def wide(ref, d):
    return jnp.concatenate(
        [
            jnp.concatenate([ref[d, 0], ref[d, 1]], axis=1),
            jnp.concatenate([ref[d, 2], ref[d, 3]], axis=1),
        ],
        axis=0,
    )


def narrow(ref):
    return jnp.concatenate(
        [jnp.concatenate([ref[4 * h + j, 4] for j in range(4)], axis=1) for h in range(2)], axis=0
    )


def reduce_kernel(
    replicas,
    all_devices,
    gq,
    eq,
    go,
    eo,
    fq,
    fo,
    giq,
    gio,
    nrm,
    mq,
    mo,
    gp_out,
    gn_out,
    norm_out,
    gq_v,
    eq_v,
    go_v,
    eo_v,
    fq_v,
    fo_v,
    giq_v,
    gio_v,
    nrm_v,
    wq,
    wo,
    send_a,
    recv_a,
    zbuf,
    gath,
    nsrc,
    nrecv,
    nz,
    nx,
    ng,
    sem_q,
    sem_o,
    sem_s,
    sem_as,
    sem_ar,
    sem_zs,
    sem_zr,
    sem_gs,
    sem_gr,
    nsem_as,
    nsem_ar,
    nsem_zs,
    nsem_zr,
    nsem_xs,
    nsem_xr,
    nsem_gs,
    nsem_gr,
):
    rep = lax.axis_index("replica")
    ten = lax.axis_index("tensor")
    nx_size = lax.axis_size("tensor")
    y = rep // (NZ * NC)
    z = (rep // NC) % NZ
    core = rep % NC
    a = y * NC + core

    def a_peer(off):
        py, pc = (y + off[0]) % NY, (core + off[1]) % NC
        return py * NC + pc, ((py * NZ + z) * NC + pc, ten)

    def z_peer(dz):
        pz = (z + dz) % NZ
        return pz, ((y * NZ + pz) * NC + core, ten)

    def x_peer(dx):
        px = (ten + dx) % nx_size
        return px, (rep, px)

    small = [(fo, fo_v), (gio, gio_v), (fq, fq_v), (giq, giq_v), (nrm, nrm_v)]
    small_copies = [pltpu.make_async_copy(s, d, sem_s.at[i]) for i, (s, d) in enumerate(small)]
    for c in small_copies:
        c.start()
    o_rows = go.shape[0] // 4
    q_rows = gq.shape[0] // NA

    def o_loads(j):
        rows = pl.ds(j * o_rows, o_rows)
        return [
            pltpu.make_async_copy(go.at[rows, :], go_v.at[rows, :], sem_o.at[0, j]),
            pltpu.make_async_copy(eo.at[rows, :], eo_v.at[rows, :], sem_o.at[1, j]),
        ]

    def q_slice(d):
        return pl.ds(pl.multiple_of(d * q_rows, q_rows), q_rows)

    def q_loads(d):
        rows = q_slice(d)
        return [
            pltpu.make_async_copy(gq.at[rows, :], gq_v.at[rows, :], sem_q.at[0, d]),
            pltpu.make_async_copy(eq.at[rows, :], eq_v.at[rows, :], sem_q.at[1, d]),
        ]

    order = A_FAR + [(0, 0)]
    for j in range(4):
        for c in o_loads(j):
            c.start()
    for off in order:
        for c in q_loads(a_peer(off)[0]):
            c.start()

    barrier = pltpu.get_barrier_semaphore()
    for off in A_FAR:
        pl.semaphore_signal(barrier, inc=1, device_id=a_peer(off)[1], device_id_type=MESH)
    for dz in Z_FAR:
        pl.semaphore_signal(barrier, inc=1, device_id=z_peer(dz)[1], device_id_type=MESH)
    for dx in range(1, nx_size):
        pl.semaphore_signal(barrier, inc=1, device_id=x_peer(dx)[1], device_id_type=MESH)

    def exchange(src, dst, send_sem, recv_sem, device):
        return pltpu.make_async_remote_copy(
            src_ref=src, dst_ref=dst, send_sem=send_sem, recv_sem=recv_sem,
            device_id=device, device_id_type=MESH,
        )

    def a_copy(ph, off):
        d, dev = a_peer(off)
        return exchange(send_a.at[ph, d], recv_a.at[ph, a], sem_as.at[ph, d], sem_ar.at[ph, a], dev)

    def a_wait(ph, off):
        d, dev = a_peer(off)
        exchange(send_a.at[ph, d], recv_a.at[ph, d], sem_as.at[ph, d], sem_ar.at[ph, d], dev).wait_recv()
        return recv_a[ph, d].astype(f32)

    def z_copy(ph, dz):
        d, dev = z_peer(dz)
        return exchange(zbuf.at[ph, z], zbuf.at[ph, z], sem_zs.at[ph, d], sem_zr.at[ph, z], dev)

    def z_wait(ph, dz):
        d, dev = z_peer(dz)
        exchange(zbuf.at[ph, d], zbuf.at[ph, d], sem_zs.at[ph, d], sem_zr.at[ph, d], dev).wait_recv()

    def g_copy(ph, off):
        d, dev = a_peer(off)
        return exchange(gath.at[ph, a], gath.at[ph, a], sem_gs.at[ph, d], sem_gr.at[ph, a], dev)

    def g_wait(ph, off):
        d, dev = a_peer(off)
        exchange(gath.at[ph, d], gath.at[ph, d], sem_gs.at[ph, d], sem_gr.at[ph, d], dev).wait_recv()
        return d

    def na_copy(off):
        d, dev = a_peer(off)
        return exchange(nsrc.at[d], nrecv.at[a], nsem_as.at[d], nsem_ar.at[a], dev)

    def na_wait(off):
        d, dev = a_peer(off)
        exchange(nsrc.at[d], nrecv.at[d], nsem_as.at[d], nsem_ar.at[d], dev).wait_recv()
        return nrecv[d]

    def nz_copy(dz):
        d, dev = z_peer(dz)
        return exchange(nz.at[z], nz.at[z], nsem_zs.at[d], nsem_zr.at[z], dev)

    def nz_wait(dz):
        d, dev = z_peer(dz)
        exchange(nz.at[d], nz.at[d], nsem_zs.at[d], nsem_zr.at[d], dev).wait_recv()

    def nx_copy(dx):
        d, dev = x_peer(dx)
        return exchange(nx.at[ten], nx.at[ten], nsem_xs.at[d], nsem_xr.at[ten], dev)

    def nx_wait(dx):
        d, dev = x_peer(dx)
        exchange(nx.at[d], nx.at[d], nsem_xs.at[d], nsem_xr.at[d], dev).wait_recv()

    def ng_copy(off):
        d, dev = a_peer(off)
        return exchange(ng.at[a], ng.at[a], nsem_gs.at[d], nsem_gr.at[a], dev)

    def ng_wait(off):
        d, dev = a_peer(off)
        exchange(ng.at[d], ng.at[d], nsem_gs.at[d], nsem_gr.at[d], dev).wait_recv()

    small_copies[0].wait()
    small_copies[1].wait()
    for i, w in enumerate(fold_gram(gio_v[...], fo_v[...])):
        wo[i * RANK : (i + 1) * RANK, :] = w
    small_copies[2].wait()
    small_copies[3].wait()
    for i, w in enumerate(fold_gram(giq_v[...], fq_v[...])):
        wq[i * RANK : (i + 1) * RANK, :] = w
    for j in range(4):
        for c in o_loads(j):
            c.wait()
        rows = pl.ds(j * o_rows, o_rows)
        mat = go_v[rows, :] + eo_v[rows, :]
        mo[rows, :] = mat
        part = project(wo[...], mat).astype(bf16)
        send_a[0, j, 4] = part[0:16]
        send_a[0, 4 + j, 4] = part[16:32]

    n_others = len(A_FAR) + len(Z_FAR) + nx_size - 1
    for i, off in enumerate(order):
        d, _ = a_peer(off)
        for c in q_loads(d):
            c.wait()
        rows = q_slice(d)
        mat = gq_v[rows, :] + eq_v[rows, :]
        mq[rows, :] = mat
        part = project(wq[...], mat).astype(bf16)
        for t, tile in enumerate(wide_tiles(part)):
            send_a[0, d, t] = tile
        if i == 0:
            pl.semaphore_wait(barrier, n_others)
        if off != (0, 0):
            a_copy(0, off).start()

    small_copies[4].wait()
    piece = nsrc.shape[2]
    for d in range(NA):
        nsrc[d] = nrm_v[0, :, d * piece : (d + 1) * piece].astype(f32)
    for off in A_FAR:
        na_copy(off).start()

    def sum_a(ph):
        total = send_a[ph, a].astype(f32)
        for off in A_NEAR:
            total = total + a_wait(ph, off)
        zbuf[ph, z] = total.astype(bf16)
        for dz in Z_FAR:
            z_copy(ph, dz).start()

    def sum_z(ph, divisor):
        for dz in Z_FAR[::-1]:
            z_wait(ph, dz)
        total = zbuf[ph, 0].astype(f32)
        for k in range(1, NZ):
            total = total + zbuf[ph, k].astype(f32)
        if divisor is not None:
            total = total / divisor
        gath[ph, a] = total.astype(bf16)
        for off in A_FAR:
            g_copy(ph, off).start()

    sum_a(0)

    ntotal = nsrc[a]
    for off in A_NEAR:
        ntotal = ntotal + na_wait(off)
    nz[z] = ntotal
    for dz in Z_FAR:
        nz_copy(dz).start()
    for off in A_FAR:
        a_copy(0, off).wait_send()

    sum_z(0, None)

    for dz in Z_FAR:
        nz_wait(dz)
    ntotal = nz[0]
    for k in range(1, NZ):
        ntotal = ntotal + nz[k]
    nx[ten] = ntotal
    for dx in range(1, nx_size):
        nx_copy(dx).start()
    for dz in Z_FAR:
        z_copy(0, dz).wait_send()
        nz_copy(dz).wait_send()
    for off in A_FAR:
        na_copy(off).wait_send()

    acc_q = jnp.zeros((RANK, mq.shape[1]), f32)
    for group in ([(0, 0)] + A_NEAR[:5], A_NEAR[5:]):
        for off in group:
            if off != (0, 0):
                g_wait(0, off)
        for off in group:
            d = a_peer(off)[0]
            acc_q = acc_q + jnp.dot(wide(gath.at[0], d), mq[q_slice(d), :], preferred_element_type=f32)
    left = narrow(gath.at[0])
    o_cols = mo.shape[1] // NA
    for d in range(NA):
        part = jnp.dot(left, mo[:, d * o_cols : (d + 1) * o_cols], preferred_element_type=f32).astype(bf16)
        for t, tile in enumerate(wide_tiles(part)):
            send_a[1, d, t] = tile
        h, j = d // 4, d % 4
        send_a[1, d, 4] = acc_q[h * 16 : h * 16 + 16, j * 128 : j * 128 + 128].astype(bf16)
    for off in A_FAR:
        a_copy(1, off).start()

    gp_out[...] = gath[0]
    for dx in range(1, nx_size):
        nx_wait(dx)
    ntotal = nx[0]
    for k in range(1, nx_size):
        ntotal = ntotal + nx[k]
    ng[a] = ntotal / all_devices
    for off in A_FAR:
        ng_copy(off).start()
    for off in A_FAR:
        g_copy(0, off).wait_send()
    for dx in range(1, nx_size):
        nx_copy(dx).wait_send()

    sum_a(1)

    for off in A_FAR:
        ng_wait(off)
    for d in range(NA):
        norm_out[:, d * piece : (d + 1) * piece] = ng[d]
    for off in A_FAR:
        a_copy(1, off).wait_send()
        ng_copy(off).wait_send()

    sum_z(1, replicas)

    for dz in Z_FAR:
        z_copy(1, dz).wait_send()
    for off in A_NEAR:
        g_wait(1, off)
    gn_out[...] = gath[1]
    for off in A_FAR:
        g_copy(1, off).wait_send()


def outer(left_t, right_t):
    return lax.dot_general(left_t, right_t, (((0,), (0,)), ((), ())), preferred_element_type=f32)


def update_kernel(
    gp, gn, nrm, mq, mo, wq, mom_q, wo, mom_o,
    eq_out, eo_out, fq_out, fo_out, momq_out, wq_out, momo_out, wo_out, norm_out,
    eq_v, eo_v, fq_v, fo_v, small_v, turn, sem_q, sem_o, sem_s,
):
    rep = lax.axis_index("replica")
    copies = []

    def put(src, dst, sem):
        c = pltpu.make_async_copy(src, dst, sem)
        c.start()
        copies.append(c)

    put(nrm, norm_out, sem_s.at[0])
    right_q = narrow(gn)
    left_o = narrow(gp)
    q_rows, o_cols = mq.shape[0] // NA, mo.shape[1] // NA
    for d in range(NA):
        rows = slice(d * q_rows, (d + 1) * q_rows)
        approx = outer(wide(gp, d), right_q)
        eq_v[rows, :] = (mq[rows, :].astype(f32) - approx).astype(bf16)
        put(eq_v.at[pl.ds(d * q_rows, q_rows), :], eq_out.at[pl.ds(d * q_rows, q_rows), :], sem_q.at[d])
    o_rows = mo.shape[0] // 4
    for d in range(NA):
        fo_v[:, d * o_cols : (d + 1) * o_cols] = wide(gn, d)
    fq_v[...] = right_q
    put(fq_v, fq_out, sem_s.at[1])
    put(fo_v, fo_out, sem_s.at[2])
    for j in range(4):
        rows = slice(j * o_rows, (j + 1) * o_rows)
        approx = outer(left_o[:, rows], fo_v[...])
        eo_v[rows, :] = (mo[rows, :].astype(f32) - approx).astype(bf16)
        put(eo_v.at[pl.ds(j * o_rows, o_rows), :], eo_out.at[pl.ds(j * o_rows, o_rows), :], sem_o.at[j])
    c = rep // 8
    off = pl.multiple_of((rep % 8) * RANK, RANK)
    turn[0] = wide(gp, c).astype(f32).T
    turn[1] = wide(gn, c).astype(f32).T
    for k, (right, mom, w) in enumerate([(right_q, mom_q, wq), (left_o, mom_o, wo)]):
        left = turn[k, pl.ds(off, RANK), :].astype(bf16)
        m = momentum_decay * mom[...] + jnp.dot(left, right, preferred_element_type=f32)
        small_v[2 * k] = m
        small_v[2 * k + 1] = w[...] - step_size * m
    for k, out in enumerate([momq_out, wq_out, momo_out, wo_out]):
        put(small_v.at[k], out, sem_s.at[3 + k])
    for c in copies:
        c.wait()


def on_device(
    grad_q,
    error_q,
    qfac_q,
    ginv_q,
    weight_q,
    momentum_q,
    grad_o,
    error_o,
    qfac_o,
    ginv_o,
    weight_o,
    momentum_o,
    norm_grads,
):
    replicas = lax.axis_size("replica")
    tensors = lax.axis_size("tensor")
    shape_q, shape_o = grad_q.shape, grad_o.shape
    piece = norm_grads.shape[2] // NA
    packed = (NA, TILES, 16, 128)
    hbm = pl.BlockSpec(memory_space=pltpu.HBM)
    vmem = pl.BlockSpec(memory_space=pltpu.VMEM)
    dma = pltpu.SemaphoreType.DMA
    mat_q, mat_o, gp, gn, norm = pl.pallas_call(
        functools.partial(reduce_kernel, replicas, replicas * tensors),
        out_shape=(
            pltpu.VMEM(shape_q, bf16),
            pltpu.VMEM(shape_o, bf16),
            pltpu.VMEM(packed, bf16),
            pltpu.VMEM(packed, bf16),
            pltpu.VMEM((1, NA * piece), f32),
        ),
        in_specs=[hbm] * 9,
        out_specs=(vmem,) * 5,
        scratch_shapes=[
            pltpu.VMEM(shape_q, bf16),
            pltpu.VMEM(shape_q, bf16),
            pltpu.VMEM(shape_o, bf16),
            pltpu.VMEM(shape_o, bf16),
            pltpu.VMEM((RANK, shape_q[1]), bf16),
            pltpu.VMEM((RANK, shape_o[1]), bf16),
            pltpu.VMEM((RANK, RANK), f32),
            pltpu.VMEM((RANK, RANK), f32),
            pltpu.VMEM(norm_grads.shape, bf16),
            pltpu.VMEM((2 * RANK, shape_q[1]), bf16),
            pltpu.VMEM((2 * RANK, shape_o[1]), bf16),
            pltpu.VMEM((2,) + packed, bf16),
            pltpu.VMEM((2,) + packed, bf16),
            pltpu.VMEM((2,) + packed, bf16),
            pltpu.VMEM((2,) + packed, bf16),
            pltpu.VMEM((NA, 1, piece), f32),
            pltpu.VMEM((NA, 1, piece), f32),
            pltpu.VMEM((NZ, 1, piece), f32),
            pltpu.VMEM((tensors, 1, piece), f32),
            pltpu.VMEM((NA, 1, piece), f32),
            dma((2, NA)),
            dma((2, 4)),
            dma((5,)),
            dma((2, NA)),
            dma((2, NA)),
            dma((2, NZ)),
            dma((2, NZ)),
            dma((2, NA)),
            dma((2, NA)),
            dma((NA,)),
            dma((NA,)),
            dma((NZ,)),
            dma((NZ,)),
            dma((tensors,)),
            dma((tensors,)),
            dma((NA,)),
            dma((NA,)),
        ],
        compiler_params=pltpu.CompilerParams(
            collective_id=0, has_side_effects=True, vmem_limit_bytes=24 << 20
        ),
        name="reduce_factors",
    )(
        *(
            pltpu.with_memory_space_constraint(x, pltpu.HBM)
            for x in (grad_q, error_q, grad_o, error_o, qfac_q.T, qfac_o.T, ginv_q, ginv_o, norm_grads)
        )
    )

    wide_piece = (RANK, shape_q[1])
    outs = pl.pallas_call(
        update_kernel,
        out_shape=(
            jax.ShapeDtypeStruct(shape_q, bf16),
            jax.ShapeDtypeStruct(shape_o, bf16),
            jax.ShapeDtypeStruct((RANK, shape_q[1]), bf16),
            jax.ShapeDtypeStruct((RANK, shape_o[1]), bf16),
            jax.ShapeDtypeStruct(wide_piece, f32),
            jax.ShapeDtypeStruct(wide_piece, f32),
            jax.ShapeDtypeStruct(wide_piece, f32),
            jax.ShapeDtypeStruct(wide_piece, f32),
            jax.ShapeDtypeStruct((1, NA * piece), f32),
        ),
        in_specs=[vmem] * 9,
        out_specs=(hbm,) * 9,
        scratch_shapes=[
            pltpu.VMEM(shape_q, bf16),
            pltpu.VMEM(shape_o, bf16),
            pltpu.VMEM((RANK, shape_q[1]), bf16),
            pltpu.VMEM((RANK, shape_o[1]), bf16),
            pltpu.VMEM((4,) + wide_piece, f32),
            pltpu.VMEM((2, 256, RANK), f32),
            dma((NA,)),
            dma((4,)),
            dma((7,)),
        ],
        compiler_params=pltpu.CompilerParams(vmem_limit_bytes=16 << 20),
        name="apply_update",
    )(gp, gn, norm, mat_q, mat_o, weight_q, momentum_q, weight_o.T, momentum_o.T)
    error_q_new, error_o_new, fq_t, fo_t, momq, wq, momo_t, wo_t, norm_mean = outs
    return (
        error_q_new,
        fq_t.T,
        momq,
        wq,
        error_o_new,
        fo_t.T,
        momo_t.T,
        wo_t.T,
        norm_mean.reshape(-1),
    )


def solution(mesh):
    in_specs = (
        P("replica", "tensor"),
        P("replica", "tensor"),
        P("tensor", None),
        P("tensor", None),
        P("replica", "tensor"),
        P("replica", "tensor"),
        P(("replica", "tensor"), None),
        P(("replica", "tensor"), None),
        P("tensor", None),
        P("tensor", None),
        P("tensor", "replica"),
        P("tensor", "replica"),
        P("replica", "tensor", None),
    )
    out_specs = (
        P("replica", "tensor"),
        P("tensor", None),
        P("replica", "tensor"),
        P("replica", "tensor"),
        P(("replica", "tensor"), None),
        P("tensor", None),
        P("tensor", "replica"),
        P("tensor", "replica"),
        P(),
    )
    return jax.shard_map(
        on_device, mesh=mesh, in_specs=in_specs, out_specs=out_specs, check_vma=False
    )
```

```python
import functools

import jax
import jax.numpy as jnp
from jax import lax
from jax.experimental import pallas as pl
from jax.experimental.pallas import tpu as pltpu
from jax.sharding import PartitionSpec as P

momentum_decay = 0.9
step_size = 0.5

NY, NZ, NC = 4, 8, 2
NA = NY * NC
RANK = 32
TILES = 5
MESH = pl.DeviceIdType.MESH
f32 = jnp.float32
bf16 = jnp.bfloat16

A_FAR = [(2, 0), (2, 1), (1, 0), (3, 0), (1, 1), (3, 1), (0, 1)]
A_NEAR = A_FAR[::-1]
Z_FAR = [4, 3, 5, 2, 6, 1, 7]
Y_FAR = [2, 1, 3, 0]


def fold_gram(gram, factor_t):
    w = lax.dot_general(
        gram,
        factor_t.astype(f32),
        (((0,), (0,)), ((), ())),
        precision=lax.Precision.HIGHEST,
        preferred_element_type=f32,
    )
    w1 = w.astype(bf16)
    return jnp.concatenate([w1, (w - w1.astype(f32)).astype(bf16)], axis=0)


def project(mat, w):
    out = lax.dot_general(w, mat, (((1,), (1,)), ((), ())), preferred_element_type=f32)
    return (out[0:RANK] + out[RANK : 2 * RANK]).astype(bf16)


def project_nn(mat, w):
    out = jnp.dot(mat, w, preferred_element_type=f32)
    return (out[:, 0:RANK] + out[:, RANK : 2 * RANK]).T.astype(bf16)


def wide_tiles(chunk):
    return [chunk[h * 16 : h * 16 + 16, j * 128 : j * 128 + 128] for h in range(2) for j in range(2)]


def wide(ref, d):
    return jnp.concatenate(
        [
            jnp.concatenate([ref[d, 0], ref[d, 1]], axis=1),
            jnp.concatenate([ref[d, 2], ref[d, 3]], axis=1),
        ],
        axis=0,
    )


def narrow(ref):
    return jnp.concatenate(
        [jnp.concatenate([ref[4 * h + j] for j in range(4)], axis=1) for h in range(2)], axis=0
    )


def reduce_kernel(
    replicas,
    all_devices,
    gq,
    eq,
    go,
    eo,
    fq,
    fo,
    giq,
    gio,
    nrm,
    mq,
    mo,
    gp_out,
    gn_out,
    norm_out,
    q_v,
    o_v,
    fq_v,
    fo_v,
    giq_v,
    gio_v,
    nrm_v,
    wq,
    wo,
    sa0,
    sa1,
    ra0,
    ra1,
    zb0,
    zb1,
    ga0,
    ga1,
    nsrc,
    nrecv,
    nz,
    nx,
    ng,
    sem_l,
    sem_s,
    sem_as,
    sem_ar,
    sem_zs,
    sem_zr,
    sem_gs,
    sem_gr,
    nsem_s,
    nsem_r,
):
    rep = lax.axis_index("replica")
    ten = lax.axis_index("tensor")
    nx_size = lax.axis_size("tensor")
    y = rep // (NZ * NC)
    z = (rep // NC) % NZ
    core = rep % NC
    a = y * NC + core

    def a_peer(off):
        py, pc = (y + off[0]) % NY, (core + off[1]) % NC
        return py * NC + pc, ((py * NZ + z) * NC + pc, ten)

    def z_peer(dz):
        pz = (z + dz) % NZ
        return pz, ((y * NZ + pz) * NC + core, ten)

    def x_peer(dx):
        px = (ten + dx) % nx_size
        return px, (rep, px)

    small = [(fo, fo_v), (gio, gio_v), (fq, fq_v), (giq, giq_v), (nrm, nrm_v)]
    small_copies = [pltpu.make_async_copy(s, d, sem_s.at[i]) for i, (s, d) in enumerate(small)]
    for c in small_copies:
        c.start()
    o_rows = go.shape[0] // 2
    q_rows = gq.shape[0] // NY

    def block(i):
        if i < 2:
            return go, eo, o_v, pl.ds(i * o_rows, o_rows)
        at = ((y + Y_FAR[i - 2]) % NY) * q_rows
        return gq, eq, q_v, pl.ds(pl.multiple_of(at, q_rows), q_rows)

    for i in range(2 + NY):
        g, e, v, rows = block(i)
        pltpu.make_async_copy(g.at[rows, :], v.at[0, rows, :], sem_l.at[i]).start()
        pltpu.make_async_copy(e.at[rows, :], v.at[1, rows, :], sem_l.at[i]).start()

    def load_sum(i, out):
        _, _, v, rows = block(i)
        both = v.at[:, rows, :]
        pltpu.make_async_copy(both, both, sem_l.at[i]).wait()
        out[rows, :] = v[0, rows, :] + v[1, rows, :]
        return rows

    barrier = pltpu.get_barrier_semaphore()
    for off in A_FAR:
        pl.semaphore_signal(barrier, inc=1, device_id=a_peer(off)[1], device_id_type=MESH)
    for dz in Z_FAR:
        pl.semaphore_signal(barrier, inc=1, device_id=z_peer(dz)[1], device_id_type=MESH)
    for dx in range(1, nx_size):
        pl.semaphore_signal(barrier, inc=1, device_id=x_peer(dx)[1], device_id_type=MESH)

    def exchange(src, dst, send_sem, recv_sem, device):
        return pltpu.make_async_remote_copy(
            src_ref=src, dst_ref=dst, send_sem=send_sem, recv_sem=recv_sem,
            device_id=device, device_id_type=MESH,
        )

    def part_of(ref, ph, d, kind):
        return ref[kind].at[ph, d]

    def wait_seven(ref, ph, kind, sem):
        seven = ref[kind].at[ph, pl.ds(0, NA - 1)]
        pltpu.make_async_copy(seven, seven, sem.at[ph, kind]).wait()

    send_a, recv_a, zbuf, gath = (sa0, sa1), (ra0, ra1), (zb0, zb1), (ga0, ga1)

    def a_send(ph, kind, offs):
        for off in offs:
            d, dev = a_peer(off)
            exchange(
                part_of(send_a, ph, d, kind), part_of(recv_a, ph, a, kind),
                sem_as.at[ph, kind], sem_ar.at[ph, kind], dev,
            ).start()

    def z_send(ph, kind):
        mine = part_of(zbuf, ph, z, kind)
        for dz in Z_FAR:
            exchange(mine, mine, sem_zs.at[ph, kind], sem_zr.at[ph, kind], z_peer(dz)[1]).start()

    def g_send(ph, kind):
        mine = part_of(gath, ph, a, kind)
        for off in A_FAR:
            exchange(mine, mine, sem_gs.at[ph, kind], sem_gr.at[ph, kind], a_peer(off)[1]).start()

    def norm_wait(ref, n, sem):
        some = ref.at[pl.ds(0, n)]
        pltpu.make_async_copy(some, some, sem).wait()

    def norm_send(src, dst, step, devices):
        for dev in devices:
            exchange(src, dst, nsem_s.at[step], nsem_r.at[step], dev).start()

    a_devices = [a_peer(off)[1] for off in A_FAR]
    z_devices = [z_peer(dz)[1] for dz in Z_FAR]
    x_devices = [x_peer(dx)[1] for dx in range(1, nx_size)]

    small_copies[0].wait()
    small_copies[1].wait()
    wo[...] = fold_gram(gio_v[...], fo_v[...]).T
    small_copies[2].wait()
    small_copies[3].wait()
    wq[...] = fold_gram(giq_v[...], fq_v[...])
    for i in range(2):
        part = project_nn(mo[load_sum(i, mo), :], wo[...])
        for j in range(2):
            for h in range(2):
                sa1[0, 4 * h + 2 * i + j] = part[16 * h : 16 * h + 16, 128 * j : 128 * j + 128]

    n_others = len(A_FAR) + len(Z_FAR) + nx_size - 1
    pl.semaphore_wait(barrier, n_others)
    a_send(0, 1, A_FAR)

    for i in range(NY):
        part = project(mq[load_sum(2 + i, mq), :], wq[...])
        for c in range(NC):
            d = ((y + Y_FAR[i]) % NY) * NC + c
            for t, tile in enumerate(wide_tiles(part[:, 256 * c : 256 * c + 256])):
                sa0[0, d, t] = tile
        a_send(0, 0, [off for off in A_FAR if off[0] == Y_FAR[i]])

    def sum_a(ph, kind):
        wait_seven(recv_a, ph, kind, sem_ar)
        total = part_of(send_a, ph, a, kind)[...].astype(f32)
        for off in A_NEAR:
            total = total + part_of(recv_a, ph, a_peer(off)[0], kind)[...].astype(f32)
        part_of(zbuf, ph, z, kind)[...] = total.astype(bf16)
        z_send(ph, kind)

    def sum_z(ph, kind, divisor):
        wait_seven(zbuf, ph, kind, sem_zr)
        total = part_of(zbuf, ph, 0, kind)[...].astype(f32)
        for k in range(1, NZ):
            total = total + part_of(zbuf, ph, k, kind)[...].astype(f32)
        if divisor is not None:
            total = total / divisor
        part_of(gath, ph, a, kind)[...] = total.astype(bf16)
        g_send(ph, kind)

    def sent(ph, kind):
        wait_seven(send_a, ph, kind, sem_as)
        wait_seven(zbuf, ph, kind, sem_zs)

    small_copies[4].wait()
    piece = nsrc.shape[2]
    for d in range(NA):
        nsrc[d] = nrm_v[0, :, d * piece : (d + 1) * piece].astype(f32)
    for off in A_FAR:
        d, dev = a_peer(off)
        norm_send(nsrc.at[d], nrecv.at[a], 0, [dev])

    sum_a(0, 1)
    sum_a(0, 0)

    norm_wait(nrecv, NA - 1, nsem_r.at[0])
    ntotal = nsrc[a]
    for off in A_NEAR:
        ntotal = ntotal + nrecv[a_peer(off)[0]]
    nz[z] = ntotal
    norm_send(nz.at[z], nz.at[z], 1, z_devices)

    sum_z(0, 1, None)

    wait_seven(gath, 0, 1, sem_gr)
    left = narrow(ga1.at[0])
    o_cols = mo.shape[1] // NA
    for d in range(NA):
        part = jnp.dot(left, mo[:, d * o_cols : (d + 1) * o_cols], preferred_element_type=f32).astype(bf16)
        for t, tile in enumerate(wide_tiles(part)):
            sa0[1, d, t] = tile
    a_send(1, 0, A_FAR)

    sum_z(0, 0, None)

    norm_wait(nz, NZ - 1, nsem_r.at[1])
    ntotal = nz[0]
    for k in range(1, NZ):
        ntotal = ntotal + nz[k]
    nx[ten] = ntotal
    norm_send(nx.at[ten], nx.at[ten], 2, x_devices)

    sum_a(1, 0)

    chunk = mq.shape[0] // NA
    wait_seven(gath, 0, 0, sem_gr)
    left = jnp.concatenate([wide(ga0.at[0], d) for d in range(NA)], axis=1)
    acc = jnp.dot(left, mq[...], preferred_element_type=f32).astype(bf16)
    for d in range(NA):
        h, j = d // 4, d % 4
        sa1[1, d] = acc[h * 16 : h * 16 + 16, j * 128 : j * 128 + 128]
    a_send(1, 1, A_FAR)

    gp_out[:, 0:4] = ga0[0]
    gp_out[:, 4] = ga1[0]
    norm_wait(nx, nx_size - 1, nsem_r.at[2])
    ntotal = nx[0]
    for k in range(1, nx_size):
        ntotal = ntotal + nx[k]
    ng[a] = ntotal / all_devices
    norm_send(ng.at[a], ng.at[a], 3, a_devices)
    norm_wait(nsrc, NA - 1, nsem_s.at[0])
    norm_wait(nz, NZ - 1, nsem_s.at[1])
    norm_wait(nx, nx_size - 1, nsem_s.at[2])

    sum_a(1, 1)
    sum_z(1, 0, replicas)

    norm_wait(ng, NA - 1, nsem_r.at[3])
    for d in range(NA):
        norm_out[:, d * piece : (d + 1) * piece] = ng[d]
    norm_wait(ng, NA - 1, nsem_s.at[3])
    for kind in range(2):
        sent(0, kind)
        wait_seven(gath, 0, kind, sem_gs)
    sent(1, 0)

    sum_z(1, 1, replicas)

    wait_seven(gath, 1, 0, sem_gr)
    gn_out[:, 0:4] = ga0[1]
    wait_seven(gath, 1, 0, sem_gs)
    sent(1, 1)
    wait_seven(gath, 1, 1, sem_gr)
    gn_out[:, 4] = ga1[1]
    wait_seven(gath, 1, 1, sem_gs)


def outer(left_t, right_t):
    return lax.dot_general(left_t, right_t, (((0,), (0,)), ((), ())), preferred_element_type=f32)


def update_kernel(
    gp, gn, nrm, mq, mo, wq, mom_q, wo, mom_o,
    eq_out, eo_out, fq_out, fo_out, momq_out, wq_out, momo_out, wo_out, norm_out,
    eq_v, eo_v, fq_v, fo_v, small_v, turn, sem_q, sem_o, sem_s,
):
    rep = lax.axis_index("replica")
    copies = []

    def put(src, dst, sem):
        c = pltpu.make_async_copy(src, dst, sem)
        c.start()
        copies.append(c)

    put(nrm, norm_out, sem_s.at[0])
    right_q = narrow(gn.at[:, 4])
    left_o = narrow(gp.at[:, 4])
    q_rows, o_cols = mq.shape[0] // NA, mo.shape[1] // NA
    for d in range(NA):
        rows = slice(d * q_rows, (d + 1) * q_rows)
        approx = outer(wide(gp, d), right_q)
        eq_v[rows, :] = (mq[rows, :].astype(f32) - approx).astype(bf16)
        put(eq_v.at[pl.ds(d * q_rows, q_rows), :], eq_out.at[pl.ds(d * q_rows, q_rows), :], sem_q.at[d])
    o_rows = mo.shape[0] // 4
    for d in range(NA):
        fo_v[:, d * o_cols : (d + 1) * o_cols] = wide(gn, d)
    fq_v[...] = right_q
    put(fq_v, fq_out, sem_s.at[1])
    put(fo_v, fo_out, sem_s.at[2])
    for j in range(4):
        rows = slice(j * o_rows, (j + 1) * o_rows)
        approx = outer(left_o[:, rows], fo_v[...])
        eo_v[rows, :] = (mo[rows, :].astype(f32) - approx).astype(bf16)
        put(eo_v.at[pl.ds(j * o_rows, o_rows), :], eo_out.at[pl.ds(j * o_rows, o_rows), :], sem_o.at[j])
    c = rep // 8
    off = pl.multiple_of((rep % 8) * RANK, RANK)
    turn[0] = wide(gp, c).astype(f32).T
    turn[1] = wide(gn, c).astype(f32).T
    for k, (right, mom, w) in enumerate([(right_q, mom_q, wq), (left_o, mom_o, wo)]):
        left = turn[k, pl.ds(off, RANK), :].astype(bf16)
        m = momentum_decay * mom[...] + jnp.dot(left, right, preferred_element_type=f32)
        small_v[2 * k] = m
        small_v[2 * k + 1] = w[...] - step_size * m
    for k, out in enumerate([momq_out, wq_out, momo_out, wo_out]):
        put(small_v.at[k], out, sem_s.at[3 + k])
    for c in copies:
        c.wait()


def on_device(
    grad_q,
    error_q,
    qfac_q,
    ginv_q,
    weight_q,
    momentum_q,
    grad_o,
    error_o,
    qfac_o,
    ginv_o,
    weight_o,
    momentum_o,
    norm_grads,
):
    replicas = lax.axis_size("replica")
    tensors = lax.axis_size("tensor")
    shape_q, shape_o = grad_q.shape, grad_o.shape
    piece = norm_grads.shape[2] // NA
    packed = (NA, TILES, 16, 128)
    hbm = pl.BlockSpec(memory_space=pltpu.HBM)
    vmem = pl.BlockSpec(memory_space=pltpu.VMEM)
    dma = pltpu.SemaphoreType.DMA
    mat_q, mat_o, gp, gn, norm = pl.pallas_call(
        functools.partial(reduce_kernel, replicas, replicas * tensors),
        out_shape=(
            pltpu.VMEM(shape_q, bf16),
            pltpu.VMEM(shape_o, bf16),
            pltpu.VMEM(packed, bf16),
            pltpu.VMEM(packed, bf16),
            pltpu.VMEM((1, NA * piece), f32),
        ),
        in_specs=[hbm] * 9,
        out_specs=(vmem,) * 5,
        scratch_shapes=[
            pltpu.VMEM((2,) + shape_q, bf16),
            pltpu.VMEM((2,) + shape_o, bf16),
            pltpu.VMEM((RANK, shape_q[1]), bf16),
            pltpu.VMEM((RANK, shape_o[1]), bf16),
            pltpu.VMEM((RANK, RANK), f32),
            pltpu.VMEM((RANK, RANK), f32),
            pltpu.VMEM(norm_grads.shape, bf16),
            pltpu.VMEM((2 * RANK, shape_q[1]), bf16),
            pltpu.VMEM((shape_o[1], 2 * RANK), bf16),
            *[pltpu.VMEM(shape, bf16) for shape in [(2, NA, 4, 16, 128), (2, NA, 16, 128)] * 4],
            pltpu.VMEM((NA, 1, piece), f32),
            pltpu.VMEM((NA, 1, piece), f32),
            pltpu.VMEM((NZ, 1, piece), f32),
            pltpu.VMEM((tensors, 1, piece), f32),
            pltpu.VMEM((NA, 1, piece), f32),
            dma((2 + NY,)),
            dma((5,)),
            *[dma((2, 2))] * 6,
            dma((4,)),
            dma((4,)),
        ],
        compiler_params=pltpu.CompilerParams(
            collective_id=0, has_side_effects=True, vmem_limit_bytes=24 << 20
        ),
        name="reduce_factors",
    )(
        *(
            pltpu.with_memory_space_constraint(x, pltpu.HBM)
            for x in (grad_q, error_q, grad_o, error_o, qfac_q.T, qfac_o.T, ginv_q, ginv_o, norm_grads)
        )
    )

    wide_piece = (RANK, shape_q[1])
    outs = pl.pallas_call(
        update_kernel,
        out_shape=(
            jax.ShapeDtypeStruct(shape_q, bf16),
            jax.ShapeDtypeStruct(shape_o, bf16),
            jax.ShapeDtypeStruct((RANK, shape_q[1]), bf16),
            jax.ShapeDtypeStruct((RANK, shape_o[1]), bf16),
            jax.ShapeDtypeStruct(wide_piece, f32),
            jax.ShapeDtypeStruct(wide_piece, f32),
            jax.ShapeDtypeStruct(wide_piece, f32),
            jax.ShapeDtypeStruct(wide_piece, f32),
            jax.ShapeDtypeStruct((1, NA * piece), f32),
        ),
        in_specs=[vmem] * 9,
        out_specs=(hbm,) * 9,
        scratch_shapes=[
            pltpu.VMEM(shape_q, bf16),
            pltpu.VMEM(shape_o, bf16),
            pltpu.VMEM((RANK, shape_q[1]), bf16),
            pltpu.VMEM((RANK, shape_o[1]), bf16),
            pltpu.VMEM((4,) + wide_piece, f32),
            pltpu.VMEM((2, 256, RANK), f32),
            dma((NA,)),
            dma((4,)),
            dma((7,)),
        ],
        compiler_params=pltpu.CompilerParams(vmem_limit_bytes=16 << 20),
        name="apply_update",
    )(gp, gn, norm, mat_q, mat_o, weight_q, momentum_q, weight_o.T, momentum_o.T)
    error_q_new, error_o_new, fq_t, fo_t, momq, wq, momo_t, wo_t, norm_mean = outs
    return (
        error_q_new,
        fq_t.T,
        momq,
        wq,
        error_o_new,
        fo_t.T,
        momo_t.T,
        wo_t.T,
        norm_mean.reshape(-1),
    )


def solution(mesh):
    in_specs = (
        P("replica", "tensor"),
        P("replica", "tensor"),
        P("tensor", None),
        P("tensor", None),
        P("replica", "tensor"),
        P("replica", "tensor"),
        P(("replica", "tensor"), None),
        P(("replica", "tensor"), None),
        P("tensor", None),
        P("tensor", None),
        P("tensor", "replica"),
        P("tensor", "replica"),
        P("replica", "tensor", None),
    )
    out_specs = (
        P("replica", "tensor"),
        P("tensor", None),
        P("replica", "tensor"),
        P("replica", "tensor"),
        P(("replica", "tensor"), None),
        P("tensor", None),
        P("tensor", "replica"),
        P("tensor", "replica"),
        P(),
    )
    return jax.shard_map(
        on_device, mesh=mesh, in_specs=in_specs, out_specs=out_specs, check_vma=False
    )
```

```python
import functools

import jax
import jax.numpy as jnp
from jax import lax
from jax.experimental import pallas as pl
from jax.experimental.pallas import tpu as pltpu
from jax.sharding import PartitionSpec as P

momentum_decay = 0.9
step_size = 0.5

NY, NZ, NC = 4, 8, 2
NA = NY * NC
RANK = 32
TILES = 5
MESH = pl.DeviceIdType.MESH
f32 = jnp.float32
bf16 = jnp.bfloat16

A_FAR = [(2, 0), (2, 1), (1, 0), (3, 0), (1, 1), (3, 1), (0, 1)]
A_NEAR = A_FAR[::-1]
Z_FAR = [4, 3, 5, 2, 6, 1, 7]
Y_FAR = [2, 1, 3, 0]


def fold_gram(gram, factor_t):
    w = lax.dot_general(
        gram,
        factor_t.astype(f32),
        (((0,), (0,)), ((), ())),
        precision=lax.Precision.HIGHEST,
        preferred_element_type=f32,
    )
    w1 = w.astype(bf16)
    return jnp.concatenate([w1, (w - w1.astype(f32)).astype(bf16)], axis=0)


def project(mat, w):
    out = lax.dot_general(w, mat, (((1,), (1,)), ((), ())), preferred_element_type=f32)
    return (out[0:RANK] + out[RANK : 2 * RANK]).astype(bf16)


def project_nn(mat, w):
    out = jnp.dot(mat, w, preferred_element_type=f32)
    return (out[:, 0:RANK] + out[:, RANK : 2 * RANK]).T.astype(bf16)


def wide_tiles(chunk):
    return [chunk[h * 16 : h * 16 + 16, j * 128 : j * 128 + 128] for h in range(2) for j in range(2)]


def wide(ref, d):
    return jnp.concatenate(
        [
            jnp.concatenate([ref[d, 0], ref[d, 1]], axis=1),
            jnp.concatenate([ref[d, 2], ref[d, 3]], axis=1),
        ],
        axis=0,
    )


def narrow(ref):
    return jnp.concatenate(
        [jnp.concatenate([ref[4 * h + j] for j in range(4)], axis=1) for h in range(2)], axis=0
    )


def reduce_kernel(
    replicas,
    all_devices,
    gq,
    eq,
    go,
    eo,
    fq,
    fo,
    giq,
    gio,
    nrm,
    mq,
    mo,
    gp_out,
    gn_out,
    norm_out,
    q_v,
    o_v,
    fq_v,
    fo_v,
    giq_v,
    gio_v,
    nrm_v,
    wq,
    wo,
    sa0,
    sa1,
    ra0,
    ra1,
    zb0,
    zb1,
    ga0,
    ga1,
    nsrc,
    nrecv,
    nz,
    nx,
    ng,
    sem_l,
    sem_s,
    sem_as,
    sem_ar,
    sem_zs,
    sem_zr,
    sem_gs,
    sem_gr,
    nsem_s,
    nsem_r,
):
    rep = lax.axis_index("replica")
    ten = lax.axis_index("tensor")
    nx_size = lax.axis_size("tensor")
    y = rep // (NZ * NC)
    z = (rep // NC) % NZ
    core = rep % NC
    a = y * NC + core

    def a_peer(off):
        py, pc = (y + off[0]) % NY, (core + off[1]) % NC
        return py * NC + pc, ((py * NZ + z) * NC + pc, ten)

    def z_peer(dz):
        pz = (z + dz) % NZ
        return pz, ((y * NZ + pz) * NC + core, ten)

    def x_peer(dx):
        px = (ten + dx) % nx_size
        return px, (rep, px)

    small = [(fo, fo_v), (gio, gio_v), (fq, fq_v), (giq, giq_v), (nrm, nrm_v)]
    small_copies = [pltpu.make_async_copy(s, d, sem_s.at[i]) for i, (s, d) in enumerate(small)]
    for c in small_copies:
        c.start()
    o_rows = go.shape[0] // 2
    q_rows = gq.shape[0] // NY

    def block(i):
        if i < 2:
            return go, eo, o_v, pl.ds(i * o_rows, o_rows)
        at = ((y + Y_FAR[i - 2]) % NY) * q_rows
        return gq, eq, q_v, pl.ds(pl.multiple_of(at, q_rows), q_rows)

    for i in range(2 + NY):
        g, e, v, rows = block(i)
        pltpu.make_async_copy(g.at[rows, :], v.at[0, rows, :], sem_l.at[i]).start()
        pltpu.make_async_copy(e.at[rows, :], v.at[1, rows, :], sem_l.at[i]).start()

    def load_sum(i, out):
        _, _, v, rows = block(i)
        both = v.at[:, rows, :]
        pltpu.make_async_copy(both, both, sem_l.at[i]).wait()
        out[rows, :] = v[0, rows, :] + v[1, rows, :]
        return rows

    barrier = pltpu.get_barrier_semaphore()
    for off in A_FAR:
        pl.semaphore_signal(barrier, inc=1, device_id=a_peer(off)[1], device_id_type=MESH)
    for dz in Z_FAR:
        pl.semaphore_signal(barrier, inc=1, device_id=z_peer(dz)[1], device_id_type=MESH)
    for dx in range(1, nx_size):
        pl.semaphore_signal(barrier, inc=1, device_id=x_peer(dx)[1], device_id_type=MESH)

    def exchange(src, dst, send_sem, recv_sem, device):
        return pltpu.make_async_remote_copy(
            src_ref=src, dst_ref=dst, send_sem=send_sem, recv_sem=recv_sem,
            device_id=device, device_id_type=MESH,
        )

    def part_of(ref, ph, d, kind):
        return ref[kind].at[ph, d]

    def wait_seven(ref, ph, kind, sem):
        seven = ref[kind].at[ph, pl.ds(0, NA - 1)]
        pltpu.make_async_copy(seven, seven, sem.at[ph, kind]).wait()

    send_a, recv_a, zbuf, gath = (sa0, sa1), (ra0, ra1), (zb0, zb1), (ga0, ga1)

    def a_send(ph, kind, offs):
        for off in offs:
            d, dev = a_peer(off)
            exchange(
                part_of(send_a, ph, d, kind), part_of(recv_a, ph, a, kind),
                sem_as.at[ph, kind], sem_ar.at[ph, kind], dev,
            ).start()

    def z_send(ph, kind):
        mine = part_of(zbuf, ph, z, kind)
        for dz in Z_FAR:
            exchange(mine, mine, sem_zs.at[ph, kind], sem_zr.at[ph, kind], z_peer(dz)[1]).start()

    def g_send(ph, kind):
        mine = part_of(gath, ph, a, kind)
        for off in A_FAR:
            exchange(mine, mine, sem_gs.at[ph, kind], sem_gr.at[ph, kind], a_peer(off)[1]).start()

    def norm_wait(ref, n, sem):
        some = ref.at[pl.ds(0, n)]
        pltpu.make_async_copy(some, some, sem).wait()

    def norm_send(src, dst, step, devices):
        for dev in devices:
            exchange(src, dst, nsem_s.at[step], nsem_r.at[step], dev).start()

    a_devices = [a_peer(off)[1] for off in A_FAR]
    z_devices = [z_peer(dz)[1] for dz in Z_FAR]
    x_devices = [x_peer(dx)[1] for dx in range(1, nx_size)]

    small_copies[0].wait()
    small_copies[1].wait()
    wo[...] = fold_gram(gio_v[...], fo_v[...]).T
    for i in range(2):
        part = project_nn(mo[load_sum(i, mo), :], wo[...])
        for j in range(2):
            for h in range(2):
                sa1[0, 4 * h + 2 * i + j] = part[16 * h : 16 * h + 16, 128 * j : 128 * j + 128]

    n_others = len(A_FAR) + len(Z_FAR) + nx_size - 1
    pl.semaphore_wait(barrier, n_others)
    a_send(0, 1, A_FAR)

    small_copies[2].wait()
    small_copies[3].wait()
    wq[...] = fold_gram(giq_v[...], fq_v[...])
    for i in range(NY):
        part = project(mq[load_sum(2 + i, mq), :], wq[...])
        for c in range(NC):
            d = ((y + Y_FAR[i]) % NY) * NC + c
            for t, tile in enumerate(wide_tiles(part[:, 256 * c : 256 * c + 256])):
                sa0[0, d, t] = tile
        a_send(0, 0, [off for off in A_FAR if off[0] == Y_FAR[i]])

    def sum_a(ph, kind):
        wait_seven(recv_a, ph, kind, sem_ar)
        total = part_of(send_a, ph, a, kind)[...].astype(f32)
        for off in A_NEAR:
            total = total + part_of(recv_a, ph, a_peer(off)[0], kind)[...].astype(f32)
        part_of(zbuf, ph, z, kind)[...] = total.astype(bf16)
        z_send(ph, kind)

    def sum_z(ph, kind, divisor):
        wait_seven(zbuf, ph, kind, sem_zr)
        total = part_of(zbuf, ph, 0, kind)[...].astype(f32)
        for k in range(1, NZ):
            total = total + part_of(zbuf, ph, k, kind)[...].astype(f32)
        if divisor is not None:
            total = total / divisor
        part_of(gath, ph, a, kind)[...] = total.astype(bf16)
        g_send(ph, kind)

    def sent(ph, kind):
        wait_seven(send_a, ph, kind, sem_as)
        wait_seven(zbuf, ph, kind, sem_zs)

    small_copies[4].wait()
    piece = nsrc.shape[2]
    for d in range(NA):
        nsrc[d] = nrm_v[0, :, d * piece : (d + 1) * piece].astype(f32)
    for off in A_FAR:
        d, dev = a_peer(off)
        norm_send(nsrc.at[d], nrecv.at[a], 0, [dev])

    sum_a(0, 1)
    sum_a(0, 0)

    norm_wait(nrecv, NA - 1, nsem_r.at[0])
    ntotal = nsrc[a]
    for off in A_NEAR:
        ntotal = ntotal + nrecv[a_peer(off)[0]]
    nz[z] = ntotal
    norm_send(nz.at[z], nz.at[z], 1, z_devices)

    sum_z(0, 1, None)

    sum_z(0, 0, None)

    wait_seven(gath, 0, 1, sem_gr)
    left = narrow(ga1.at[0])
    o_cols = mo.shape[1] // NA
    for dy in Y_FAR:
        d = ((y + dy) % NY) * NC
        cols = pl.ds(pl.multiple_of(d * o_cols, NC * o_cols), NC * o_cols)
        part = jnp.dot(left, mo[:, cols], preferred_element_type=f32).astype(bf16)
        for c in range(NC):
            for t, tile in enumerate(wide_tiles(part[:, c * o_cols : (c + 1) * o_cols])):
                sa0[1, d + c, t] = tile
        a_send(1, 0, [off for off in A_FAR if off[0] == dy])

    norm_wait(nz, NZ - 1, nsem_r.at[1])
    ntotal = nz[0]
    for k in range(1, NZ):
        ntotal = ntotal + nz[k]
    nx[ten] = ntotal
    norm_send(nx.at[ten], nx.at[ten], 2, x_devices)

    chunk = mq.shape[0] // NA
    wait_seven(gath, 0, 0, sem_gr)
    left = jnp.concatenate([wide(ga0.at[0], d) for d in range(NA)], axis=1)
    acc = jnp.dot(left, mq[...], preferred_element_type=f32).astype(bf16)
    for d in range(NA):
        h, j = d // 4, d % 4
        sa1[1, d] = acc[h * 16 : h * 16 + 16, j * 128 : j * 128 + 128]
    a_send(1, 1, A_FAR)

    sum_a(1, 0)

    gp_out[:, 0:4] = ga0[0]
    gp_out[:, 4] = ga1[0]
    norm_wait(nx, nx_size - 1, nsem_r.at[2])
    ntotal = nx[0]
    for k in range(1, nx_size):
        ntotal = ntotal + nx[k]
    ng[a] = ntotal / all_devices
    norm_send(ng.at[a], ng.at[a], 3, a_devices)
    norm_wait(nsrc, NA - 1, nsem_s.at[0])
    norm_wait(nz, NZ - 1, nsem_s.at[1])
    norm_wait(nx, nx_size - 1, nsem_s.at[2])

    sum_a(1, 1)
    sum_z(1, 0, replicas)

    norm_wait(ng, NA - 1, nsem_r.at[3])
    for d in range(NA):
        norm_out[:, d * piece : (d + 1) * piece] = ng[d]
    norm_wait(ng, NA - 1, nsem_s.at[3])
    for kind in range(2):
        sent(0, kind)
        wait_seven(gath, 0, kind, sem_gs)
    sent(1, 0)

    sum_z(1, 1, replicas)

    wait_seven(gath, 1, 0, sem_gr)
    gn_out[:, 0:4] = ga0[1]
    wait_seven(gath, 1, 0, sem_gs)
    sent(1, 1)
    wait_seven(gath, 1, 1, sem_gr)
    gn_out[:, 4] = ga1[1]
    wait_seven(gath, 1, 1, sem_gs)


def outer(left_t, right_t):
    return lax.dot_general(left_t, right_t, (((0,), (0,)), ((), ())), preferred_element_type=f32)


def update_kernel(
    gp, gn, nrm, mq, mo, wq, mom_q, wo, mom_o,
    eq_out, eo_out, fq_out, fo_out, momq_out, wq_out, momo_out, wo_out, norm_out,
    eq_v, eo_v, fq_v, fo_v, small_v, turn, sem_q, sem_o, sem_s,
):
    rep = lax.axis_index("replica")
    copies = []

    def put(src, dst, sem):
        c = pltpu.make_async_copy(src, dst, sem)
        c.start()
        copies.append(c)

    put(nrm, norm_out, sem_s.at[0])
    right_q = narrow(gn.at[:, 4])
    left_o = narrow(gp.at[:, 4])
    q_rows, o_cols = mq.shape[0] // NA, mo.shape[1] // NA
    for d in range(NA):
        rows = slice(d * q_rows, (d + 1) * q_rows)
        approx = outer(wide(gp, d), right_q)
        eq_v[rows, :] = (mq[rows, :].astype(f32) - approx).astype(bf16)
        put(eq_v.at[pl.ds(d * q_rows, q_rows), :], eq_out.at[pl.ds(d * q_rows, q_rows), :], sem_q.at[d])
    o_rows = mo.shape[0] // 4
    for d in range(NA):
        fo_v[:, d * o_cols : (d + 1) * o_cols] = wide(gn, d)
    fq_v[...] = right_q
    put(fq_v, fq_out, sem_s.at[1])
    put(fo_v, fo_out, sem_s.at[2])
    for j in range(4):
        rows = slice(j * o_rows, (j + 1) * o_rows)
        approx = outer(left_o[:, rows], fo_v[...])
        eo_v[rows, :] = (mo[rows, :].astype(f32) - approx).astype(bf16)
        put(eo_v.at[pl.ds(j * o_rows, o_rows), :], eo_out.at[pl.ds(j * o_rows, o_rows), :], sem_o.at[j])
    c = rep // 8
    off = pl.multiple_of((rep % 8) * RANK, RANK)
    turn[0] = wide(gp, c).astype(f32).T
    turn[1] = wide(gn, c).astype(f32).T
    for k, (right, mom, w) in enumerate([(right_q, mom_q, wq), (left_o, mom_o, wo)]):
        left = turn[k, pl.ds(off, RANK), :].astype(bf16)
        m = momentum_decay * mom[...] + jnp.dot(left, right, preferred_element_type=f32)
        small_v[2 * k] = m
        small_v[2 * k + 1] = w[...] - step_size * m
    for k, out in enumerate([momq_out, wq_out, momo_out, wo_out]):
        put(small_v.at[k], out, sem_s.at[3 + k])
    for c in copies:
        c.wait()


def on_device(
    grad_q,
    error_q,
    qfac_q,
    ginv_q,
    weight_q,
    momentum_q,
    grad_o,
    error_o,
    qfac_o,
    ginv_o,
    weight_o,
    momentum_o,
    norm_grads,
):
    replicas = lax.axis_size("replica")
    tensors = lax.axis_size("tensor")
    shape_q, shape_o = grad_q.shape, grad_o.shape
    piece = norm_grads.shape[2] // NA
    packed = (NA, TILES, 16, 128)
    hbm = pl.BlockSpec(memory_space=pltpu.HBM)
    vmem = pl.BlockSpec(memory_space=pltpu.VMEM)
    dma = pltpu.SemaphoreType.DMA
    mat_q, mat_o, gp, gn, norm = pl.pallas_call(
        functools.partial(reduce_kernel, replicas, replicas * tensors),
        out_shape=(
            pltpu.VMEM(shape_q, bf16),
            pltpu.VMEM(shape_o, bf16),
            pltpu.VMEM(packed, bf16),
            pltpu.VMEM(packed, bf16),
            pltpu.VMEM((1, NA * piece), f32),
        ),
        in_specs=[hbm] * 9,
        out_specs=(vmem,) * 5,
        scratch_shapes=[
            pltpu.VMEM((2,) + shape_q, bf16),
            pltpu.VMEM((2,) + shape_o, bf16),
            pltpu.VMEM((RANK, shape_q[1]), bf16),
            pltpu.VMEM((RANK, shape_o[1]), bf16),
            pltpu.VMEM((RANK, RANK), f32),
            pltpu.VMEM((RANK, RANK), f32),
            pltpu.VMEM(norm_grads.shape, bf16),
            pltpu.VMEM((2 * RANK, shape_q[1]), bf16),
            pltpu.VMEM((shape_o[1], 2 * RANK), bf16),
            *[pltpu.VMEM(shape, bf16) for shape in [(2, NA, 4, 16, 128), (2, NA, 16, 128)] * 4],
            pltpu.VMEM((NA, 1, piece), f32),
            pltpu.VMEM((NA, 1, piece), f32),
            pltpu.VMEM((NZ, 1, piece), f32),
            pltpu.VMEM((tensors, 1, piece), f32),
            pltpu.VMEM((NA, 1, piece), f32),
            dma((2 + NY,)),
            dma((5,)),
            *[dma((2, 2))] * 6,
            dma((4,)),
            dma((4,)),
        ],
        compiler_params=pltpu.CompilerParams(
            collective_id=0, has_side_effects=True, vmem_limit_bytes=24 << 20
        ),
        name="reduce_factors",
    )(
        *(
            pltpu.with_memory_space_constraint(x, pltpu.HBM)
            for x in (grad_q, error_q, grad_o, error_o, qfac_q.T, qfac_o.T, ginv_q, ginv_o, norm_grads)
        )
    )

    wide_piece = (RANK, shape_q[1])
    outs = pl.pallas_call(
        update_kernel,
        out_shape=(
            jax.ShapeDtypeStruct(shape_q, bf16),
            jax.ShapeDtypeStruct(shape_o, bf16),
            jax.ShapeDtypeStruct((RANK, shape_q[1]), bf16),
            jax.ShapeDtypeStruct((RANK, shape_o[1]), bf16),
            jax.ShapeDtypeStruct(wide_piece, f32),
            jax.ShapeDtypeStruct(wide_piece, f32),
            jax.ShapeDtypeStruct(wide_piece, f32),
            jax.ShapeDtypeStruct(wide_piece, f32),
            jax.ShapeDtypeStruct((1, NA * piece), f32),
        ),
        in_specs=[vmem] * 9,
        out_specs=(hbm,) * 9,
        scratch_shapes=[
            pltpu.VMEM(shape_q, bf16),
            pltpu.VMEM(shape_o, bf16),
            pltpu.VMEM((RANK, shape_q[1]), bf16),
            pltpu.VMEM((RANK, shape_o[1]), bf16),
            pltpu.VMEM((4,) + wide_piece, f32),
            pltpu.VMEM((2, 256, RANK), f32),
            dma((NA,)),
            dma((4,)),
            dma((7,)),
        ],
        compiler_params=pltpu.CompilerParams(vmem_limit_bytes=16 << 20),
        name="apply_update",
    )(gp, gn, norm, mat_q, mat_o, weight_q, momentum_q, weight_o.T, momentum_o.T)
    error_q_new, error_o_new, fq_t, fo_t, momq, wq, momo_t, wo_t, norm_mean = outs
    return (
        error_q_new,
        fq_t.T,
        momq,
        wq,
        error_o_new,
        fo_t.T,
        momo_t.T,
        wo_t.T,
        norm_mean.reshape(-1),
    )


def solution(mesh):
    in_specs = (
        P("replica", "tensor"),
        P("replica", "tensor"),
        P("tensor", None),
        P("tensor", None),
        P("replica", "tensor"),
        P("replica", "tensor"),
        P(("replica", "tensor"), None),
        P(("replica", "tensor"), None),
        P("tensor", None),
        P("tensor", None),
        P("tensor", "replica"),
        P("tensor", "replica"),
        P("replica", "tensor", None),
    )
    out_specs = (
        P("replica", "tensor"),
        P("tensor", None),
        P("replica", "tensor"),
        P("replica", "tensor"),
        P(("replica", "tensor"), None),
        P("tensor", None),
        P("tensor", "replica"),
        P("tensor", "replica"),
        P(),
    )
    return jax.shard_map(
        on_device, mesh=mesh, in_specs=in_specs, out_specs=out_specs, check_vma=False
    )
```
